32 devices in a mesh: tm: 16 (over z, x, core), head: 2 (over y).
Axes of the slice: x: 2, y: 2, z: 4, core: 2. Of those that a mesh axis runs over, the one named last changes fastest.
Arguments:
- queries: bfloat16 [16, 392, 1024], P('tm', None, 'head'), may hold values from -6 to 6
- key_tokens: bfloat16 [16, 392, 1024], P('tm', None, 'head'), may hold values from -6 to 6
- value_tokens: bfloat16 [16, 392, 1024], P('tm', None, 'head'), may hold values from -6 to 6
- out_weight: bfloat16 [1024, 1024], P('head'), may hold values from -0.1875 to 0.1875
- out_grad: bfloat16 [16, 392, 1024], P('tm'), may hold values from -6 to 6
- clip_starts: int32 [16], P('tm'), may hold values from 0 to 1, as said below
Outputs:
- projected: bfloat16 [16, 392, 1024], P('tm', 'head')
- grad_queries: bfloat16 [16, 392, 1024], P('tm', None, 'head')
- grad_keys: bfloat16 [16, 392, 1024], P('tm', None, 'head')
- grad_values: bfloat16 [16, 392, 1024], P('tm', None, 'head')
The draws below stay inside these ranges and needn't reach their ends.
Inputs may be any that keep to these rules, and one draw needn't show every extreme that they name: `clip_starts`: the last 8 clips never begin a new video.
All inputs are finite; a program needn't handle non-finite values.
Results may differ from the reference program's by a relative error of at most 0.0087.
Values may be sent and summed in bfloat16 or wider, within the bound.
A program may use at most 64 MiB of HBM per device.

```python
import jax
import jax.numpy as jnp
from jax import lax

HEADS = 16
HEAD_DIM = 64
WIDTH = 1024
TOK = 392
POOL = 4
MEM = 8
CLIPS = 16


def base_field(key, seed_tag):
    return jax.random.truncated_normal(jax.random.fold_in(key, seed_tag), -6.0, 6.0, (CLIPS, TOK, WIDTH), jnp.float32)


def draw_queries(key, part):
    field = base_field(key, 1)
    return field.astype(jnp.bfloat16)


def draw_key_tokens(key, part):
    field = base_field(key, 2)
    return field.astype(jnp.bfloat16)


def draw_clip_starts(key, part):
    dice = jax.random.randint(jax.random.fold_in(key, 21), (CLIPS,), 0, 4)
    forced = jax.random.randint(jax.random.fold_in(key, 22), (), 0, CLIPS - MEM)
    positions = jnp.arange(CLIPS)
    starts = jnp.where((dice == 0) | (positions == forced), 1, 0).astype(jnp.int32)
    late = positions >= CLIPS - MEM
    return jnp.where(late, 0, starts).astype(jnp.int32)


def levels(own_key, shape, pieces, least, high):
    loudness = 1.0
    for dim, parts in pieces:
        steps = jax.random.uniform(jax.random.fold_in(jax.random.fold_in(own_key, 6), dim), (parts,), jnp.float32, least / len(pieces), high / len(pieces))
        loudness = loudness * jnp.repeat(jnp.exp(steps), shape[dim] // parts).reshape((-1,) + (1,) * (len(shape) - 1 - dim))
    return loudness


def noise(key, shape, deviation, reach, pieces=(), held_as=jnp.bfloat16):
    loudness = levels(key, shape, pieces, -0.22, 0.18) if pieces else 1.0
    result = jax.random.normal(key, shape, jnp.float32) * deviation * loudness
    return jnp.minimum(jnp.maximum(result, -reach), reach).astype(held_as)


def setup_inputs(seed: int = 0) -> dict:
    key_list = jax.random.split(jax.random.key(seed), 7)
    return {
        "queries": draw_queries(jax.random.fold_in(key_list[6], 71), 0),
        "key_tokens": draw_key_tokens(jax.random.fold_in(key_list[6], 71), 0),
        "value_tokens": noise(key_list[2], (CLIPS, TOK, WIDTH), 1.0, 6.0, ((0, 16), (2, 2))),
        "out_weight": noise(key_list[3], (WIDTH, WIDTH), WIDTH ** -0.5, 0.1875, ((0, 2),)),
        "out_grad": noise(key_list[4], (CLIPS, TOK, WIDTH), 1.0, 6.0, ((0, 16),)),
        "clip_starts": draw_clip_starts(jax.random.fold_in(key_list[6], 71), 0),
    }


def delayed(series, places):
    return jnp.concatenate([jnp.zeros((places,), series.dtype), series[:series.shape[0] - places]])


def clip_terms(query_clip, key_ext, value_ext, column_mask, grad_clip):
    scale = HEAD_DIM ** -0.5
    query_heads = query_clip.astype(jnp.float32).reshape(TOK, HEADS, HEAD_DIM)
    key_heads = key_ext.astype(jnp.float32).reshape(-1, HEADS, HEAD_DIM)
    value_heads = value_ext.astype(jnp.float32).reshape(-1, HEADS, HEAD_DIM)
    grad_heads = grad_clip.astype(jnp.float32).reshape(TOK, HEADS, HEAD_DIM)
    scores = jnp.einsum('qhd,khd->hqk', query_heads, key_heads) * scale
    scores = jnp.where(column_mask[None, None, :] > 0, scores, -1e30)
    peak = jnp.max(scores, axis=-1, keepdims=True)
    expo = jnp.exp(scores - peak)
    probs = expo / jnp.sum(expo, axis=-1, keepdims=True)
    weights = lax.optimization_barrier(probs.astype(jnp.bfloat16)).astype(jnp.float32)
    attended = jnp.einsum('hqk,khd->qhd', weights, value_heads).reshape(TOK, WIDTH).astype(jnp.bfloat16)
    grad_probs = jnp.einsum('qhd,khd->hqk', grad_heads, value_heads)
    delta = jnp.sum(probs * grad_probs, axis=-1, keepdims=True)
    grad_scores = (probs * (grad_probs - delta) * scale).astype(jnp.bfloat16)
    grad_scores = lax.optimization_barrier(grad_scores).astype(jnp.float32)
    grad_query = jnp.einsum('hqk,khd->qhd', grad_scores, key_heads).reshape(TOK, WIDTH).astype(jnp.bfloat16)
    grad_key = jnp.einsum('hqk,qhd->khd', grad_scores, query_heads).reshape(-1, WIDTH)
    grad_value = jnp.einsum('hqk,qhd->khd', weights, grad_heads).reshape(-1, WIDTH)
    return attended, grad_query, grad_key, grad_value


def reference(queries, key_tokens, value_tokens, out_weight, out_grad, clip_starts):
    clips = queries.shape[0]
    pooled_count = TOK // POOL
    pooled_keys = key_tokens.astype(jnp.float32).reshape(clips, pooled_count, POOL, WIDTH).mean(axis=2).astype(jnp.bfloat16)
    pooled_values = value_tokens.astype(jnp.float32).reshape(clips, pooled_count, POOL, WIDTH).mean(axis=2).astype(jnp.bfloat16)
    keep = (1 - clip_starts).astype(jnp.float32)
    present = jnp.ones((clips,), jnp.float32)
    running = keep
    allowed_list = []
    for distance in range(1, MEM + 1):
        allowed_list.append(running * delayed(present, distance))
        running = running * delayed(keep, distance)
    allowed = jnp.stack(allowed_list, axis=1)
    grad_attended = jnp.dot(out_grad.reshape(clips * TOK, WIDTH), out_weight.T, preferred_element_type=jnp.float32)
    grad_attended = grad_attended.astype(jnp.bfloat16).reshape(clips, TOK, WIDTH)
    sources = jnp.maximum(jnp.arange(clips)[:, None] - jnp.arange(1, MEM + 1)[None, :], 0).astype(jnp.int32)

    def per_clip(position):
        memory_keys = pooled_keys[sources[position]].reshape(MEM * pooled_count, WIDTH)
        memory_values = pooled_values[sources[position]].reshape(MEM * pooled_count, WIDTH)
        key_ext = jnp.concatenate([key_tokens[position], memory_keys], axis=0)
        value_ext = jnp.concatenate([value_tokens[position], memory_values], axis=0)
        column_mask = jnp.concatenate([jnp.ones((TOK,), jnp.float32), jnp.repeat(allowed[position], pooled_count)])
        return clip_terms(queries[position], key_ext, value_ext, column_mask, grad_attended[position])

    attended, grad_queries, grad_key_ext, grad_value_ext = lax.map(per_clip, jnp.arange(clips))
    memory_key_grads = grad_key_ext[:, TOK:].reshape(clips, MEM, pooled_count, WIDTH)
    memory_value_grads = grad_value_ext[:, TOK:].reshape(clips, MEM, pooled_count, WIDTH)
    returned_keys = jnp.zeros((clips, pooled_count, WIDTH), jnp.float32)
    returned_values = jnp.zeros((clips, pooled_count, WIDTH), jnp.float32)
    for distance in range(1, MEM + 1):
        padding = jnp.zeros((distance, pooled_count, WIDTH), jnp.float32)
        returned_keys = returned_keys + jnp.concatenate([memory_key_grads[distance:, distance - 1], padding], axis=0)
        returned_values = returned_values + jnp.concatenate([memory_value_grads[distance:, distance - 1], padding], axis=0)
    grad_keys = (grad_key_ext[:, :TOK] + jnp.repeat(returned_keys, POOL, axis=1) / POOL).astype(jnp.bfloat16)
    grad_values = (grad_value_ext[:, :TOK] + jnp.repeat(returned_values, POOL, axis=1) / POOL).astype(jnp.bfloat16)
    projected = jnp.dot(attended.reshape(clips * TOK, WIDTH), out_weight, preferred_element_type=jnp.float32)
    projected = projected.astype(jnp.bfloat16).reshape(clips, TOK, WIDTH)
    return projected, grad_queries, grad_keys, grad_values
```

```python
import functools

import jax
import jax.numpy as jnp
from jax import lax
from jax.experimental import pallas as pl
from jax.experimental.pallas import tpu as pltpu
from jax.sharding import PartitionSpec as P

HEAD_DIM = 64
POOL = 4
MEM = 8
GROUP = 4
LANES = 2 * HEAD_DIM
EXCLUDED = -1e30
F32 = jnp.float32
BF16 = jnp.bfloat16
BY_COLUMN = (((1,), (1,)), ((), ()))
BY_ROW = (((0,), (0,)), ((), ()))


def attention_kernel(
    start, q_ref, k_ref, v_ref, mem_ref, weight_ref, grad_ref,
    share_ref, dq_ref, own_ref, memory_grad_ref,
    key_ext, value_ext, bias, partial_ref,
):
    step = pl.program_id(0)
    tokens = q_ref.shape[0]
    pooled = tokens // POOL
    pitch = mem_ref.shape[2]
    base = MEM * pitch
    extent = key_ext.shape[0]

    @pl.when(step == 0)
    def _():
        bias[...] = jnp.full(bias.shape, EXCLUDED, BF16)
        running = jnp.full((1, LANES), 1 - start[0], jnp.int32).astype(F32)
        for slot in range(MEM):
            keep = mem_ref[slot, 0, pooled : pooled + 1, :].astype(F32)
            exists = mem_ref[slot, 0, pooled + 1 : pooled + 2, :].astype(F32)
            level = ((1.0 - running * exists) * EXCLUDED).astype(BF16)
            bias[slot * pitch : slot * pitch + pooled, :] = jnp.broadcast_to(level, (pooled, LANES))
            running = running * keep
        bias[base : base + tokens, :] = jnp.zeros((tokens, LANES), BF16)
        key_ext[base + tokens :, :] = jnp.zeros((extent - base - tokens, LANES), BF16)
        value_ext[base + tokens :, :] = jnp.zeros((extent - base - tokens, LANES), BF16)

    for slot in range(MEM):
        rows = slice(slot * pitch, (slot + 1) * pitch)
        key_ext[rows, :] = mem_ref[slot, 0]
        value_ext[rows, :] = mem_ref[slot, 1]
    key_ext[base : base + tokens, :] = k_ref[...]
    value_ext[base : base + tokens, :] = v_ref[...]

    scale = HEAD_DIM ** (-0.5)
    grad_t = lax.dot_general(weight_ref[...], grad_ref[...], BY_COLUMN, preferred_element_type=F32)
    query = q_ref[...]
    keys = key_ext[...]
    values = value_ext[...]
    key_t = keys.T
    value_t = values.T
    query_t = (query * scale).T
    token_lane = lax.broadcasted_iota(jnp.int32, (tokens, LANES), 1)
    ext_lane = lax.broadcasted_iota(jnp.int32, keys.shape, 1)
    ones = jnp.ones((16, extent), BF16)
    line = lax.broadcasted_iota(jnp.int32, (HEAD_DIM, tokens), 0)
    attended, dq, dk, dv = [], [], [], []
    for side in range(2):
        mine = (token_lane < HEAD_DIM) if side == 0 else (token_lane >= HEAD_DIM)
        mine_ext = (ext_lane < HEAD_DIM) if side == 0 else (ext_lane >= HEAD_DIM)
        head = slice(side * HEAD_DIM, (side + 1) * HEAD_DIM)
        spare = HEAD_DIM * (1 - side)
        query_aug = jnp.where(mine, query, jnp.where(token_lane == spare, 1.0, 0.0).astype(BF16))
        key_aug = jnp.where(mine_ext, keys, bias[...])
        value_aug = jnp.where(mine_ext, values, jnp.ones_like(values))
        scores = lax.dot_general(query_aug, key_aug, BY_COLUMN, preferred_element_type=F32)
        peak = jnp.max(scores, axis=1, keepdims=True)
        expo = jnp.exp((scores - peak) * scale)
        expo_low = expo.astype(BF16)
        moving = jnp.concatenate([value_t[head, :], ones], axis=0)
        gathered = lax.dot_general(moving, expo_low, BY_COLUMN, preferred_element_type=F32)
        inverse = 1.0 / gathered[HEAD_DIM : HEAD_DIM + 1, :]
        attended_side = gathered[:HEAD_DIM, :] * inverse
        grad_side = (grad_t[head, :] * inverse).astype(BF16)
        delta = jnp.sum(grad_side.astype(F32) * attended_side, axis=0, keepdims=True)
        high = delta.astype(BF16).astype(F32)
        low = delta - high
        extra = jnp.where(line == 0, -high, jnp.where(line == 1, -low, 0.0)).astype(BF16)
        pair = [grad_side, extra] if side == 0 else [extra, grad_side]
        grad_aug = jnp.concatenate(pair, axis=0).T
        centred = lax.dot_general(grad_aug, value_aug, BY_COLUMN, preferred_element_type=F32)
        grad_scores = (expo * centred).astype(BF16)
        dv.append(jnp.dot(grad_side, expo_low, preferred_element_type=F32))
        dk.append(jnp.dot(query_t[head, :], grad_scores, preferred_element_type=F32))
        dq.append(lax.dot_general(key_t[head, :], grad_scores, BY_COLUMN, preferred_element_type=F32))
        attended.append(attended_side)
    dq_ref[...] = (jnp.concatenate(dq, axis=0) * scale).astype(BF16).T
    for which, parts in enumerate((dk, dv)):
        total = jnp.concatenate(parts, axis=0)
        memory = total[:, : base].astype(BF16).T
        for slot in range(MEM):
            memory_grad_ref[slot, which] = memory[slot * pitch : (slot + 1) * pitch, :]
        own_ref[which] = total[:, base : ].T[:tokens, :]
    share = jnp.dot(
        jnp.concatenate(attended, axis=0).astype(BF16).T, weight_ref[...], preferred_element_type=F32
    )

    @pl.when(step == 0)
    def _():
        partial_ref[...] = share

    @pl.when(step > 0)
    def _():
        partial_ref[...] += share

    @pl.when(step == pl.num_programs(0) - 1)
    def _():
        rows = share_ref.shape[1]
        for part in range(share_ref.shape[0]):
            share_ref[part] = partial_ref[part * rows : (part + 1) * rows, :].astype(BF16)


def attention(start, queries, keys, values, memory, weight, grad, parts):
    tokens, width = queries.shape
    full = weight.shape[1]
    pitch = memory.shape[2]
    extent = -(-(MEM * pitch + tokens) // LANES) * LANES
    columns = pl.BlockSpec((tokens, LANES), lambda i: (0, i))
    memory_block = pl.BlockSpec((MEM, 2, pitch, LANES), lambda i: (0, 0, 0, i))
    return pl.pallas_call(
        attention_kernel,
        grid=(width // LANES,),
        in_specs=[
            pl.BlockSpec(memory_space=pltpu.SMEM),
            columns,
            columns,
            columns,
            memory_block,
            pl.BlockSpec((LANES, full), lambda i: (i, 0)),
            pl.BlockSpec((tokens, full), lambda i: (0, 0)),
        ],
        out_specs=[
            pl.BlockSpec((parts, tokens // parts, full), lambda i: (0, 0, 0)),
            columns,
            pl.BlockSpec((2, tokens, LANES), lambda i: (0, 0, i)),
            memory_block,
        ],
        out_shape=[
            jax.ShapeDtypeStruct((parts, tokens // parts, full), BF16),
            jax.ShapeDtypeStruct((tokens, width), BF16),
            jax.ShapeDtypeStruct((2, tokens, width), F32),
            jax.ShapeDtypeStruct((MEM, 2, pitch, width), BF16),
        ],
        scratch_shapes=[pltpu.VMEM((extent, LANES), BF16)] * 3 + [pltpu.VMEM((tokens, full), F32)],
        compiler_params=pltpu.CompilerParams(dimension_semantics=("arbitrary",)),
        name="attention",
    )(start, queries, keys, values, memory, weight, grad)


def remote(source, target, send, receive, device):
    return pltpu.make_async_remote_copy(
        src_ref=source,
        dst_ref=target,
        send_sem=send,
        recv_sem=receive,
        device_id=device,
        device_id_type=pl.DeviceIdType.MESH,
    )


def place(count):
    me = lax.axis_index("tm")
    core = lax.rem(me, 2)
    side = lax.rem(me // 2, 2)
    sibling = {"tm": me + 1 - 2 * core}
    across = {"tm": me + 2 - 4 * side}
    later = {"tm": lax.rem(me + GROUP, count)}
    earlier = {"tm": lax.rem(me + count - GROUP, count)}
    return me, core, side, sibling, across, later, earlier, me + GROUP < count, me >= GROUP


def greet(neighbours):
    barrier = pltpu.get_barrier_semaphore()
    for device in neighbours:
        pl.semaphore_signal(
            barrier, inc=1, device_id=device, device_id_type=pl.DeviceIdType.MESH
        )
    pl.semaphore_wait(barrier, len(neighbours))


def gather_kernel(count, start, k_ref, v_ref, out_ref, buf, send, receive, stored):
    me, core, side, sibling, across, later, earlier, has_later, has_earlier = place(count)
    tokens, width = k_ref.shape
    pooled = tokens // POOL
    pitch = out_ref.shape[2]
    row = lax.broadcasted_iota(jnp.int32, (pitch, tokens), 0)
    token = lax.broadcasted_iota(jnp.int32, (pitch, tokens), 1)
    inside = (token >= row * POOL) & (token < row * POOL + POOL)
    mixing = jnp.where(inside, 1.0 / POOL, 0.0).astype(BF16)
    line = lax.broadcasted_iota(jnp.int32, (pitch, width), 0)
    keep = jnp.full((pitch, width), 1 - start[0], jnp.int32).astype(F32)
    for which, ref in enumerate((k_ref, v_ref)):
        mean = jnp.dot(mixing, ref[...], preferred_element_type=F32)
        mean = jnp.where(line == pooled, keep, jnp.where(line == pooled + 1, 1.0, mean))
        buf[0, which] = mean.astype(BF16)

    @pl.when(jnp.logical_not(has_earlier))
    def _():
        for slot in (4, 8):
            buf[slot] = jnp.zeros(buf.shape[1:], BF16)

    greet([sibling, across, later, earlier])

    def move(source, target, which, number, device):
        return remote(
            buf.at[source, which], buf.at[target, which],
            send.at[number, which], receive.at[target, which], device,
        )

    def arrive(slot, which):
        move(slot, slot, which, 0, sibling).wait_recv()

    def store(slot, which):
        pltpu.make_async_copy(
            buf.at[slot, which], out_ref.at[slot - 1, which], stored.at[slot - 1, which]
        ).start()

    for which in range(2):
        pl.when(has_later)(lambda: move(0, 4, which, 0, later).start())
        pl.when(side == 0)(lambda: move(0, 2, which, 2, across).start())
        pl.when(core == 0)(lambda: move(0, 1, which, 4, sibling).start())
    for which in range(2):
        pl.when(has_earlier)(lambda: arrive(4, which))
        pl.when(has_later)(lambda: move(4, 8, which, 1, later).start())
        pl.when(side == 0)(lambda: move(4, 6, which, 3, across).start())
        pl.when(side == 1)(lambda: move(4, 2, which, 2, across).start())
        pl.when(core == 0)(lambda: move(4, 5, which, 5, sibling).start())
        pl.when(core == 1)(lambda: move(4, 3, which, 4, sibling).start())
        store(4, which)
    for which in range(2):
        arrive(2, which)
        pl.when(core == 0)(lambda: move(2, 3, which, 6, sibling).start())
        pl.when(core == 1)(lambda: move(2, 1, which, 6, sibling).start())
        store(2, which)
    for which in range(2):
        pl.when(has_earlier)(lambda: arrive(8, which))
        pl.when(side == 1)(lambda: move(8, 6, which, 3, across).start())
        pl.when(core == 1)(lambda: move(8, 7, which, 5, sibling).start())
        store(8, which)
    for which in range(2):
        arrive(6, which)
        pl.when(core == 0)(lambda: move(6, 7, which, 7, sibling).start())
        pl.when(core == 1)(lambda: move(6, 5, which, 7, sibling).start())
        store(6, which)
    for slot in (1, 3, 5, 7):
        for which in range(2):
            arrive(slot, which)
            store(slot, which)
    for which in range(2):
        for number in (0, 1):
            pl.when(has_later)(lambda: move(0, 4, which, number, later).wait_send())
        for number in range(2, 8):
            move(0, 2, which, number, across).wait_send()
        for slot in range(1, MEM + 1):
            pltpu.make_async_copy(
                buf.at[slot, which], out_ref.at[slot - 1, which], stored.at[slot - 1, which]
            ).wait()


def gather(start, keys, values, count):
    tokens, width = keys.shape
    pitch = -(-(tokens // POOL + 2) // 8) * 8
    whole = pl.BlockSpec(memory_space=pltpu.VMEM)
    return pl.pallas_call(
        functools.partial(gather_kernel, count),
        in_specs=[pl.BlockSpec(memory_space=pltpu.SMEM), whole, whole],
        out_specs=pl.BlockSpec(memory_space=pl.ANY),
        out_shape=jax.ShapeDtypeStruct((MEM, 2, pitch, width), BF16),
        scratch_shapes=[
            pltpu.VMEM((MEM + 1, 2, pitch, width), BF16),
            pltpu.SemaphoreType.DMA((8, 2)),
            pltpu.SemaphoreType.DMA((MEM + 1, 2)),
            pltpu.SemaphoreType.DMA((MEM, 2)),
        ],
        compiler_params=pltpu.CompilerParams(collective_id=1, has_side_effects=True),
        name="gather",
    )(start, keys, values)


def giving_kernel(
    count, parts, grads, share_ref, projected_ref, returned_ref,
    landed, sums, shares, send, receive, share_send, share_receive,
):
    me, core, side, sibling, across, later, earlier, has_later, has_earlier = place(count)
    head = lax.axis_index("head")

    @pl.when(jnp.logical_not(has_later))
    def _():
        for number in (6, 7):
            landed[number] = jnp.zeros(landed.shape[1:], BF16)

    peers = [{"head": lax.rem(head + k, parts)} for k in range(1, parts)]
    greet([sibling, across, later, earlier] + peers)

    def move(source, number, which, device):
        return remote(
            source, landed.at[number, which],
            send.at[number, which], receive.at[number, which], device,
        )

    def slot(index, which):
        return grads.at[index - 1, which]

    for which in range(2):
        for number, bottom, step in ((3, 5, 2), (1, 7, -2), (2, 1, 2), (0, 3, -2)):
            move(slot(bottom + step * core, which), number, which, sibling).start()
    exchanges = []
    for k, peer in enumerate(peers):
        copy = remote(
            share_ref.at[lax.rem(head + k + 1, parts)], shares.at[k],
            share_send.at[k], share_receive.at[k], peer,
        )
        copy.start()
        exchanges.append(copy)

    def arrive(number, which):
        move(slot(1, which), number, which, sibling).wait_recv()
        return landed[number, which].astype(F32)

    is_core = core.astype(F32)
    is_side = side.astype(F32)
    for which in range(2):
        sums[1, which] = (grads[5, which].astype(F32) + arrive(3, which)).astype(BF16)
        move(sums.at[1, which], 5, which, across).start()
    for which in range(2):
        from_core = arrive(1, which)
        sums[0, which] = (grads[1, which].astype(F32) + arrive(2, which)).astype(BF16)
        move(sums.at[0, which], 4, which, across).start()
    for which in range(2):
        total = grads[7, which].astype(F32) + is_core * landed[1, which].astype(F32)
        total = total + is_side * arrive(5, which)
        sums[3, which] = total.astype(BF16)
        pl.when(has_earlier)(lambda: move(sums.at[3, which], 7, which, earlier).start())
    for which in range(2):
        total = grads[3, which].astype(F32) + (1 - is_core) * landed[1, which].astype(F32)
        total = total + is_core * arrive(0, which)
        total = total + (1 - is_side) * landed[5, which].astype(F32)
        total = total + is_side * arrive(4, which)
        pl.when(has_later)(
            lambda: move(slot(1, which), 7, which, sibling).wait_recv()
        )
        total = total + landed[7, which].astype(F32)
        sums[2, which] = total.astype(BF16)
        pl.when(has_earlier)(lambda: move(sums.at[2, which], 6, which, earlier).start())

    for copy in exchanges:
        copy.wait()
    projected = share_ref[head].astype(F32)
    for k in range(parts - 1):
        projected = projected + shares[k].astype(F32)
    projected_ref[...] = projected.astype(BF16)

    for which in range(2):
        pl.when(has_later)(
            lambda: move(slot(1, which), 6, which, sibling).wait_recv()
        )
        total = (1 - is_core) * landed[0, which].astype(F32) + landed[6, which].astype(F32)
        total = total + (1 - is_side) * landed[4, which].astype(F32)
        returned_ref[which] = total.astype(BF16)
    for which in range(2):
        for number in range(6):
            move(slot(1, which), number, which, sibling).wait_send()
        for number in (6, 7):
            pl.when(has_earlier)(
                lambda: move(slot(1, which), number, which, sibling).wait_send()
            )


def give_back(grads, share, count):
    parts, rows, full = share.shape
    pitch, width = grads.shape[2:]
    whole = pl.BlockSpec(memory_space=pltpu.VMEM)
    return pl.pallas_call(
        functools.partial(giving_kernel, count, parts),
        in_specs=[whole] * 2,
        out_specs=[whole] * 2,
        out_shape=[
            jax.ShapeDtypeStruct((rows, full), BF16),
            jax.ShapeDtypeStruct((2, pitch, width), BF16),
        ],
        scratch_shapes=[
            pltpu.VMEM((8, 2, pitch, width), BF16),
            pltpu.VMEM((4, 2, pitch, width), BF16),
            pltpu.VMEM((parts - 1, rows, full), BF16),
            pltpu.SemaphoreType.DMA((8, 2)),
            pltpu.SemaphoreType.DMA((8, 2)),
            pltpu.SemaphoreType.DMA((parts - 1,)),
            pltpu.SemaphoreType.DMA((parts - 1,)),
        ],
        compiler_params=pltpu.CompilerParams(collective_id=2, has_side_effects=True),
        name="give_back",
    )(grads, share)


def finish_kernel(own_ref, returned_ref, share_ref, projected_ref, dk_ref, dv_ref):
    tokens = own_ref.shape[1]
    pitch = returned_ref.shape[1]
    token = lax.broadcasted_iota(jnp.int32, (tokens, pitch), 0)
    row = lax.broadcasted_iota(jnp.int32, (tokens, pitch), 1)
    inside = (token >= row * POOL) & (token < row * POOL + POOL)
    spread = jnp.where(inside, 1.0 / POOL, 0.0).astype(BF16)
    for which, ref in enumerate((dk_ref, dv_ref)):
        shared = jnp.dot(spread, returned_ref[which], preferred_element_type=F32)
        ref[...] = (own_ref[which] + shared).astype(BF16)
    projected_ref[...] = share_ref[...]


def finish(own, returned, share):
    _, tokens, width = own.shape
    pitch = returned.shape[1]
    rows, full = share.shape
    steps = width // LANES
    columns = pl.BlockSpec((tokens, LANES), lambda i: (0, i))
    shares = pl.BlockSpec((rows, full // steps), lambda i: (0, i))
    return pl.pallas_call(
        finish_kernel,
        grid=(steps,),
        in_specs=[
            pl.BlockSpec((2, tokens, LANES), lambda i: (0, 0, i)),
            pl.BlockSpec((2, pitch, LANES), lambda i: (0, 0, i)),
            shares,
        ],
        out_specs=[shares, columns, columns],
        out_shape=[
            jax.ShapeDtypeStruct((rows, full), BF16),
            jax.ShapeDtypeStruct((tokens, width), BF16),
            jax.ShapeDtypeStruct((tokens, width), BF16),
        ],
        compiler_params=pltpu.CompilerParams(dimension_semantics=("arbitrary",)),
        name="finish",
    )(own, returned, share)


def local(queries, key_tokens, value_tokens, out_weight, out_grad, clip_starts):
    count = lax.axis_size("tm")
    memory = gather(clip_starts, key_tokens[0], value_tokens[0], count)
    share, dq, own, memory_grads = attention(
        clip_starts, queries[0], key_tokens[0], value_tokens[0], memory, out_weight, out_grad[0],
        lax.axis_size("head"),
    )
    share, returned = give_back(memory_grads, share, count)
    projected, dk, dv = finish(own, returned, share)
    return (projected[None], dq[None], dk[None], dv[None])


def solution(mesh):
    return jax.shard_map(
        local,
        mesh=mesh,
        in_specs=(
            P("tm", None, "head"),
            P("tm", None, "head"),
            P("tm", None, "head"),
            P("head", None),
            P("tm", None, None),
            P("tm"),
        ),
        out_specs=(
            P("tm", "head", None),
            P("tm", None, "head"),
            P("tm", None, "head"),
            P("tm", None, "head"),
        ),
        check_vma=False,
    )
```

```python
import functools

import jax
import jax.numpy as jnp
from jax import lax
from jax.experimental import pallas as pl
from jax.experimental.pallas import tpu as pltpu
from jax.sharding import PartitionSpec as P

HEAD_DIM = 64
POOL = 4
MEM = 8
GROUP = 4
LANES = 2 * HEAD_DIM
EXCLUDED = -1e30
F32 = jnp.float32
BF16 = jnp.bfloat16
BY_COLUMN = (((1,), (1,)), ((), ()))


def remote(source, target, send, receive, device):
    return pltpu.make_async_remote_copy(
        src_ref=source,
        dst_ref=target,
        send_sem=send,
        recv_sem=receive,
        device_id=device,
        device_id_type=pl.DeviceIdType.MESH,
    )


def place(count):
    me = lax.axis_index("tm")
    core = lax.rem(me, 2)
    side = lax.rem(me // 2, 2)
    sibling = {"tm": me + 1 - 2 * core}
    across = {"tm": me + 2 - 4 * side}
    later = {"tm": lax.rem(me + GROUP, count)}
    earlier = {"tm": lax.rem(me + count - GROUP, count)}
    return me, core, side, sibling, across, later, earlier, me + GROUP < count, me >= GROUP


def kernel(
    count, parts, start, q_in, k_in, v_in, weight_in, grad_in,
    projected, dq_out, dk_out, dv_out,
    q, k, v, grad, weights, mem, key_ext, value_ext, bias, grad_t,
    own, grads, landed, sums, att, att_in, dq_buf, out_buf, projected_buf,
    loads, gsend, greceive, bsend, breceive, wsend, wreceive, fsend, freceive,
    asend, areceive, stores,
):
    me, core, side, sibling, across, later, earlier, has_later, has_earlier = place(count)
    head = lax.axis_index("head")
    tokens, width = q.shape
    full = grad.shape[1]
    chunks = width // LANES
    pooled = tokens // POOL
    pitch = mem.shape[3]
    base = MEM * pitch
    extent = key_ext.shape[0]
    rows = tokens // parts
    half = width // 2
    scale = HEAD_DIM ** (-0.5)

    def load(number, source, target):
        return pltpu.make_async_copy(source, target, loads.at[number])

    inputs = [
        load(0, k_in, k), load(1, v_in, v), load(2, weight_in, weights.at[head]),
        load(3, grad_in, grad), load(4, q_in, q),
    ]
    for copy in inputs:
        copy.start()

    peers = [{"head": lax.rem(head + n, parts)} for n in range(1, parts)]
    barrier = pltpu.get_barrier_semaphore()
    neighbours = [sibling, across, later, earlier] + peers
    for device in neighbours:
        pl.semaphore_signal(barrier, inc=1, device_id=device, device_id_type=pl.DeviceIdType.MESH)

    row = lax.broadcasted_iota(jnp.int32, (pitch, tokens), 0)
    token = lax.broadcasted_iota(jnp.int32, (pitch, tokens), 1)
    inside = (token >= row * POOL) & (token < row * POOL + POOL)
    mixing = jnp.where(inside, 1.0 / POOL, 0.0).astype(BF16)
    line = lax.broadcasted_iota(jnp.int32, (pitch, width), 0)
    keep = jnp.full((pitch, width), 1 - start[0], jnp.int32).astype(F32)
    for which, ref in enumerate((k, v)):
        inputs[which].wait()
        mean = jnp.dot(mixing, ref[...], preferred_element_type=F32)
        mean = jnp.where(line == pooled, keep, jnp.where(line == pooled + 1, 1.0, mean)).astype(BF16)
        for c in range(chunks):
            mem[c, 0, which] = mean[:, c * LANES : (c + 1) * LANES]

    @pl.when(jnp.logical_not(has_earlier))
    def _():
        for slot in (4, 8):
            for c in range(chunks):
                mem[c, slot] = jnp.zeros(mem.shape[2:], BF16)

    @pl.when(jnp.logical_not(has_later))
    def _():
        for number in (6, 7):
            for c in range(chunks):
                landed[c, number] = jnp.zeros(landed.shape[2:], BF16)

    pl.semaphore_wait(barrier, len(neighbours))

    def move(c, source, target, number, device):
        return remote(
            mem.at[c, source], mem.at[c, target],
            gsend.at[c, number], greceive.at[c, target], device,
        )

    def arrive(c, slot):
        move(c, slot, slot, 0, sibling).wait_recv()

    def send_own(c):
        pl.when(has_later)(lambda: move(c, 0, 4, 0, later).start())
        pl.when(side == 0)(lambda: move(c, 0, 2, 2, across).start())
        pl.when(core == 0)(lambda: move(c, 0, 1, 4, sibling).start())

    def relay_four(c):
        pl.when(has_earlier)(lambda: arrive(c, 4))
        pl.when(has_later)(lambda: move(c, 4, 8, 1, later).start())
        move(c, 4, 6 - 4 * side, 3 - side, across).start()
        move(c, 4, 5 - 2 * core, 5 - core, sibling).start()

    def relay_two_and_eight(c):
        arrive(c, 2)
        move(c, 2, 3 - 2 * core, 6, sibling).start()
        pl.when(has_earlier)(lambda: arrive(c, 8))
        pl.when(side == 1)(lambda: move(c, 8, 6, 3, across).start())
        pl.when(core == 1)(lambda: move(c, 8, 7, 5, sibling).start())

    def relay_six(c):
        arrive(c, 6)
        move(c, 6, 7 - 2 * core, 7, sibling).start()

    def gathered_all(c):
        for slot in (1, 3, 5, 7):
            arrive(c, slot)

    def gather_sent(c):
        for number in (0, 1):
            pl.when(has_later)(lambda: move(c, 0, 4, number, later).wait_send())
        for number in range(2, 8):
            move(c, 0, 2, number, across).wait_send()

    def give(c, source, number, device):
        return remote(
            source, landed.at[c, number], bsend.at[c, number], breceive.at[c, number], device
        )

    def got(c, number):
        give(c, grads.at[c, 0], number, sibling).wait_recv()

    is_core = core.astype(F32)
    is_side = side.astype(F32)

    def term(c, number):
        return landed[c, number].astype(F32)

    def give_siblings(c):
        for number, bottom, step in ((3, 5, 2), (1, 7, -2), (2, 1, 2), (0, 3, -2)):
            give(c, grads.at[c, bottom + step * core - 1], number, sibling).start()

    def give_across(c):
        got(c, 3)
        sums[c, 1] = (grads[c, 5].astype(F32) + term(c, 3)).astype(BF16)
        give(c, sums.at[c, 1], 5, across).start()
        got(c, 2)
        sums[c, 0] = (grads[c, 1].astype(F32) + term(c, 2)).astype(BF16)
        give(c, sums.at[c, 0], 4, across).start()

    def give_eight(c):
        got(c, 1)
        got(c, 5)
        total = grads[c, 7].astype(F32) + is_core * term(c, 1) + is_side * term(c, 5)
        sums[c, 3] = total.astype(BF16)
        pl.when(has_earlier)(lambda: give(c, sums.at[c, 3], 7, earlier).start())

    def give_four(c):
        got(c, 0)
        got(c, 4)
        total = grads[c, 3].astype(F32) + (1 - is_core) * term(c, 1) + is_core * term(c, 0)
        total = total + (1 - is_side) * term(c, 5) + is_side * term(c, 4)
        pl.when(has_later)(lambda: got(c, 7))
        total = total + term(c, 7)
        sums[c, 2] = total.astype(BF16)
        pl.when(has_earlier)(lambda: give(c, sums.at[c, 2], 6, earlier).start())

    def columns(c):
        return pl.ds(pl.multiple_of(c * LANES, LANES), LANES)

    def store(c, number, source, target):
        return pltpu.make_async_copy(source, target.at[:, columns(c)], stores.at[c, number])

    spread_token = lax.broadcasted_iota(jnp.int32, (tokens, pitch), 0)
    spread_row = lax.broadcasted_iota(jnp.int32, (tokens, pitch), 1)
    spread_inside = (spread_token >= spread_row * POOL) & (spread_token < spread_row * POOL + POOL)

    def finish(c):
        pl.when(has_later)(lambda: got(c, 6))
        total = (1 - is_core) * term(c, 0) + term(c, 6) + (1 - is_side) * term(c, 4)
        total = total.astype(BF16)
        spread = jnp.where(spread_inside, 1.0 / POOL, 0.0).astype(BF16)
        for which, target in enumerate((dk_out, dv_out)):
            shared = jnp.dot(spread, total[which], preferred_element_type=F32)
            out_buf[c, which] = (own[c, which] + shared).astype(BF16)
            store(c, which, out_buf.at[c, which], target).start()

    def given(c):
        for number in range(6):
            give(c, grads.at[c, 0], number, sibling).wait_send()
        for number in (6, 7):
            pl.when(has_earlier)(lambda: give(c, grads.at[c, 0], number, sibling).wait_send())

    def weight_out(n):
        mine = weights.at[head, pl.ds(core * half, half)]
        return remote(mine, mine, wsend.at[n - 1], wreceive.at[n - 1], peers[n - 1])

    def weight_on(n):
        theirs = weights.at[lax.rem(head + parts - n, parts), pl.ds(core * half, half)]
        return remote(theirs, theirs, fsend.at[n - 1], freceive.at[n - 1], sibling)

    def attended_out(c, n):
        return remote(
            att.at[lax.rem(head + n, parts), :, columns(c)], att_in.at[head, :, columns(c)],
            asend.at[c, n - 1], areceive.at[c, n - 1], peers[n - 1],
        )

    send_own(0)
    if chunks > 1:
        send_own(1)
    inputs[2].wait()
    for n in range(1, parts):
        weight_out(n).start()
    relay_four(0)
    inputs[3].wait()
    grad_t[...] = lax.dot_general(
        weights[head], grad[...], BY_COLUMN, preferred_element_type=F32
    ).reshape(grad_t.shape)
    relay_two_and_eight(0)
    bias[...] = jnp.full(bias.shape, EXCLUDED, BF16)
    bias[base : base + tokens, :] = jnp.zeros((tokens, LANES), BF16)
    key_ext[base + tokens :, :] = jnp.zeros((extent - base - tokens, LANES), BF16)
    value_ext[base + tokens :, :] = jnp.zeros((extent - base - tokens, LANES), BF16)
    inputs[4].wait()
    relay_six(0)
    gathered_all(0)
    running = jnp.full((1, LANES), 1 - start[0], jnp.int32).astype(F32)
    for slot in range(MEM):
        keep_slot = mem[0, slot + 1, 0, pooled : pooled + 1, :].astype(F32)
        exists = mem[0, slot + 1, 0, pooled + 1 : pooled + 2, :].astype(F32)
        level = ((1.0 - running * exists) * EXCLUDED).astype(BF16)
        bias[slot * pitch : slot * pitch + pooled, :] = jnp.broadcast_to(level, (pooled, LANES))
        running = running * keep_slot

    def step(i, carry):
        @pl.when(i > 0)
        def _():
            gathered_all(i)
            give_across(i - 1)

        @pl.when(i + 1 < chunks)
        def _():
            relay_four(i + 1)

        for slot in range(MEM):
            lines = slice(slot * pitch, (slot + 1) * pitch)
            key_ext[lines, :] = mem[i, slot + 1, 0]
            value_ext[lines, :] = mem[i, slot + 1, 1]
        key_ext[base : base + tokens, :] = k[:, columns(i)]
        value_ext[base : base + tokens, :] = v[:, columns(i)]

        token_lane = lax.broadcasted_iota(jnp.int32, (tokens, LANES), 1)
        ext_lane = lax.broadcasted_iota(jnp.int32, (extent, LANES), 1)
        ones = jnp.ones((16, extent), BF16)
        extra_line = lax.broadcasted_iota(jnp.int32, (HEAD_DIM, tokens), 0)
        query = q[:, columns(i)]
        query_t = (query * scale).T
        keys = key_ext[...]
        values = value_ext[...]
        key_t = keys.T
        value_t = values.T
        attended, dq, dk, dv = [], [], [], []
        for which_head in range(2):
            mine = (token_lane < HEAD_DIM) if which_head == 0 else (token_lane >= HEAD_DIM)
            mine_ext = (ext_lane < HEAD_DIM) if which_head == 0 else (ext_lane >= HEAD_DIM)
            lines = slice(which_head * HEAD_DIM, (which_head + 1) * HEAD_DIM)
            spare = HEAD_DIM * (1 - which_head)
            query_aug = jnp.where(mine, query, jnp.where(token_lane == spare, 1.0, 0.0).astype(BF16))
            key_aug = jnp.where(mine_ext, keys, bias[...])
            value_aug = jnp.where(mine_ext, values, jnp.ones_like(values))
            scores = lax.dot_general(query_aug, key_aug, BY_COLUMN, preferred_element_type=F32)
            peak = jnp.max(scores, axis=1, keepdims=True)
            expo = jnp.exp((scores - peak) * scale)
            expo_low = expo.astype(BF16)
            moving = jnp.concatenate([value_t[lines, :], ones], axis=0)
            gathered = lax.dot_general(moving, expo_low, BY_COLUMN, preferred_element_type=F32)
            inverse = 1.0 / gathered[HEAD_DIM : HEAD_DIM + 1, :]
            attended_side = gathered[:HEAD_DIM, :] * inverse
            grad_side = (grad_t[i, lines, :] * inverse).astype(BF16)
            delta = jnp.sum(grad_side.astype(F32) * attended_side, axis=0, keepdims=True)
            high = delta.astype(BF16).astype(F32)
            low = delta - high
            extra = jnp.where(extra_line == 0, -high, jnp.where(extra_line == 1, -low, 0.0)).astype(BF16)
            pair = [grad_side, extra] if which_head == 0 else [extra, grad_side]
            grad_aug = jnp.concatenate(pair, axis=0).T
            centred = lax.dot_general(grad_aug, value_aug, BY_COLUMN, preferred_element_type=F32)
            grad_scores = (expo * centred).astype(BF16)
            dv.append(jnp.dot(grad_side, expo_low, preferred_element_type=F32))
            dk.append(jnp.dot(query_t[lines, :], grad_scores, preferred_element_type=F32))
            dq.append(lax.dot_general(key_t[lines, :], grad_scores, BY_COLUMN, preferred_element_type=F32))
            attended.append(attended_side)
            if which_head == 0:
                @pl.when(i > 0)
                def _():
                    give_eight(i - 1)

                @pl.when(i + 1 < chunks)
                def _():
                    relay_two_and_eight(i + 1)

        totals = [jnp.concatenate(pair, axis=0) for pair in (dk, dv)]
        for which, total in enumerate(totals):
            memory = total[:, :base].astype(BF16).T
            for slot in range(MEM):
                grads[i, slot, which] = memory[slot * pitch : (slot + 1) * pitch, :]
        attended = jnp.concatenate(attended, axis=0).astype(BF16).T
        for part in range(parts):
            att[part, :, columns(i)] = attended[part * rows : (part + 1) * rows, :]
        give_siblings(i)
        for n in range(1, parts):
            attended_out(i, n).start()

        @pl.when(i > 0)
        def _():
            give_four(i - 1)

        @pl.when(i + 1 < chunks)
        def _():
            relay_six(i + 1)

        @pl.when(i + 2 < chunks)
        def _():
            send_own(i + 2)

        for which, total in enumerate(totals):
            own[i, which] = total[:, base:].T[:tokens, :]
        dq_buf[i] = (jnp.concatenate(dq, axis=0) * scale).astype(BF16).T
        store(i, 2, dq_buf.at[i], dq_out).start()

        @pl.when(i > 0)
        def _():
            finish(i - 1)

        @pl.when(i == min(1, chunks - 1))
        def _():
            for n in range(1, parts):
                weight_out(n).wait_recv()
                weight_on(n).start()

        gather_sent(i)
        return carry

    lax.fori_loop(0, chunks, step, 0)

    last = chunks - 1
    give_across(last)
    total = jnp.dot(att[head], weights[head], preferred_element_type=F32)
    for n in range(1, parts):
        weight_on(n).wait_recv()
        for c in range(chunks):
            attended_out(c, n).wait_recv()
    give_eight(last)
    for n in range(1, parts):
        other = lax.rem(head + n, parts)
        total = total + jnp.dot(att_in[other], weights[other], preferred_element_type=F32)
    projected_buf[...] = total.astype(BF16)
    final = pltpu.make_async_copy(projected_buf, projected, loads.at[5])
    final.start()
    give_four(last)
    for c in range(chunks - 1):
        given(c)
        for number in range(3):
            store(c, number, dq_buf.at[c], dq_out).wait()
    for n in range(1, parts):
        weight_out(n).wait_send()
        weight_on(n).wait_send()
        for c in range(chunks):
            attended_out(c, n).wait_send()
    finish(last)
    given(last)
    for number in range(3):
        store(last, number, dq_buf.at[last], dq_out).wait()
    final.wait()


def whole(queries, key_tokens, value_tokens, out_weight, out_grad, start, count, parts):
    tokens, width = queries.shape
    full = out_weight.shape[1]
    chunks = width // LANES
    rows = tokens // parts
    pitch = -(-(tokens // POOL + 2) // 8) * 8
    extent = -(-(MEM * pitch + tokens) // LANES) * LANES
    anywhere = pl.BlockSpec(memory_space=pl.ANY)
    dma = pltpu.SemaphoreType.DMA
    return pl.pallas_call(
        functools.partial(kernel, count, parts),
        in_specs=[pl.BlockSpec(memory_space=pltpu.SMEM)] + [anywhere] * 5,
        out_specs=[anywhere] * 4,
        out_shape=[
            jax.ShapeDtypeStruct((rows, full), BF16),
            jax.ShapeDtypeStruct((tokens, width), BF16),
            jax.ShapeDtypeStruct((tokens, width), BF16),
            jax.ShapeDtypeStruct((tokens, width), BF16),
        ],
        scratch_shapes=[
            pltpu.VMEM((tokens, width), BF16),
            pltpu.VMEM((tokens, width), BF16),
            pltpu.VMEM((tokens, width), BF16),
            pltpu.VMEM((tokens, full), BF16),
            pltpu.VMEM((parts, width, full), BF16),
            pltpu.VMEM((chunks, MEM + 1, 2, pitch, LANES), BF16),
            pltpu.VMEM((extent, LANES), BF16),
            pltpu.VMEM((extent, LANES), BF16),
            pltpu.VMEM((extent, LANES), BF16),
            pltpu.VMEM((chunks, LANES, tokens), F32),
            pltpu.VMEM((chunks, 2, tokens, LANES), F32),
            pltpu.VMEM((chunks, MEM, 2, pitch, LANES), BF16),
            pltpu.VMEM((chunks, 8, 2, pitch, LANES), BF16),
            pltpu.VMEM((chunks, 4, 2, pitch, LANES), BF16),
            pltpu.VMEM((parts, rows, width), BF16),
            pltpu.VMEM((parts, rows, width), BF16),
            pltpu.VMEM((chunks, tokens, LANES), BF16),
            pltpu.VMEM((chunks, 2, tokens, LANES), BF16),
            pltpu.VMEM((rows, full), BF16),
            dma((6,)),
            dma((chunks, 8)),
            dma((chunks, MEM + 1)),
            dma((chunks, 8)),
            dma((chunks, 8)),
            dma((parts - 1,)),
            dma((parts - 1,)),
            dma((parts - 1,)),
            dma((parts - 1,)),
            dma((chunks, parts - 1)),
            dma((chunks, parts - 1)),
            dma((chunks, 3)),
        ],
        compiler_params=pltpu.CompilerParams(collective_id=1, has_side_effects=True),
        name="attention",
    )(start, queries, key_tokens, value_tokens, out_weight, out_grad)


def local(queries, key_tokens, value_tokens, out_weight, out_grad, clip_starts):
    projected, dq, dk, dv = whole(
        queries[0], key_tokens[0], value_tokens[0], out_weight, out_grad[0], clip_starts,
        lax.axis_size("tm"), lax.axis_size("head"),
    )
    return (projected[None], dq[None], dk[None], dv[None])


def solution(mesh):
    return jax.shard_map(
        local,
        mesh=mesh,
        in_specs=(
            P("tm", None, "head"),
            P("tm", None, "head"),
            P("tm", None, "head"),
            P("head", None),
            P("tm", None, None),
            P("tm"),
        ),
        out_specs=(
            P("tm", "head", None),
            P("tm", None, "head"),
            P("tm", None, "head"),
            P("tm", None, "head"),
        ),
        check_vma=False,
    )
```

```python
import functools

import jax
import jax.numpy as jnp
from jax import lax
from jax.experimental import pallas as pl
from jax.experimental.pallas import tpu as pltpu
from jax.sharding import PartitionSpec as P

HEAD_DIM = 64
POOL = 4
MEM = 8
GROUP = 4
LANES = 2 * HEAD_DIM
EXCLUDED = -1e30
F32 = jnp.float32
BF16 = jnp.bfloat16
BY_COLUMN = (((1,), (1,)), ((), ()))


def remote(source, target, send, receive, device):
    return pltpu.make_async_remote_copy(
        src_ref=source,
        dst_ref=target,
        send_sem=send,
        recv_sem=receive,
        device_id=device,
        device_id_type=pl.DeviceIdType.MESH,
    )


def place(count):
    me = lax.axis_index("tm")
    core = lax.rem(me, 2)
    side = lax.rem(me // 2, 2)
    sibling = {"tm": me + 1 - 2 * core}
    across = {"tm": me + 2 - 4 * side}
    later = {"tm": lax.rem(me + GROUP, count)}
    earlier = {"tm": lax.rem(me + count - GROUP, count)}
    return me, core, side, sibling, across, later, earlier, me + GROUP < count, me >= GROUP


def kernel(
    count, parts, start, q_in, k_in, v_in, weight_in, grad_in,
    projected, dq_out, dk_out, dv_out,
    q, k, v, grad, weights, mem, keys, values, bias, grad_t,
    query_t, key_own_t, own_probs, own_out, own_peak, own_grad, dq_part,
    own, grads, landed, sums, totals, att, att_in, dq_buf, out_buf, projected_buf,
    loads, gsend, greceive, bsend, breceive, wsend, wreceive, fsend, freceive,
    asend, areceive, stores,
):
    me, core, side, sibling, across, later, earlier, has_later, has_earlier = place(count)
    head = lax.axis_index("head")
    tokens, width = q.shape
    full = grad.shape[1]
    chunks = width // LANES
    pooled = tokens // POOL
    pitch = mem.shape[3]
    base = MEM * pitch
    rows = tokens // parts
    half = width // 2
    scale = HEAD_DIM ** (-0.5)

    def load(number, source, target):
        return pltpu.make_async_copy(source, target, loads.at[number])

    inputs = [
        load(0, k_in, k), load(1, v_in, v), load(2, weight_in, weights.at[head]),
        load(3, grad_in, grad), load(4, q_in, q),
    ]
    for copy in inputs:
        copy.start()

    peers = [{"head": lax.rem(head + n, parts)} for n in range(1, parts)]
    barrier = pltpu.get_barrier_semaphore()
    neighbours = [sibling, across, later, earlier] + peers
    for device in neighbours:
        pl.semaphore_signal(barrier, inc=1, device_id=device, device_id_type=pl.DeviceIdType.MESH)

    row = lax.broadcasted_iota(jnp.int32, (pitch, tokens), 0)
    token = lax.broadcasted_iota(jnp.int32, (pitch, tokens), 1)
    inside = (token >= row * POOL) & (token < row * POOL + POOL)
    mixing = jnp.where(inside, 1.0 / POOL, 0.0).astype(BF16)
    line = lax.broadcasted_iota(jnp.int32, (pitch, width), 0)
    keep = jnp.full((pitch, width), 1 - start[0], jnp.int32).astype(F32)
    for which, ref in enumerate((k, v)):
        inputs[which].wait()
        mean = jnp.dot(mixing, ref[...], preferred_element_type=F32)
        mean = jnp.where(line == pooled, keep, jnp.where(line == pooled + 1, 1.0, mean)).astype(BF16)
        for c in range(chunks):
            mem[c, 0, which] = mean[:, c * LANES : (c + 1) * LANES]

    @pl.when(jnp.logical_not(has_earlier))
    def _():
        for slot in (4, 8):
            for c in range(chunks):
                mem[c, slot] = jnp.zeros(mem.shape[2:], BF16)

    @pl.when(jnp.logical_not(has_later))
    def _():
        for number in (6, 7):
            for c in range(chunks):
                landed[c, number] = jnp.zeros(landed.shape[2:], BF16)

    pl.semaphore_wait(barrier, len(neighbours))

    def move(c, source, target, number, device):
        return remote(
            mem.at[c, source], mem.at[c, target],
            gsend.at[c, number], greceive.at[c, target], device,
        )

    def arrive(c, slot):
        move(c, slot, slot, 0, sibling).wait_recv()

    def send_own(c):
        pl.when(has_later)(lambda: move(c, 0, 4, 0, later).start())
        pl.when(side == 0)(lambda: move(c, 0, 2, 2, across).start())
        pl.when(core == 0)(lambda: move(c, 0, 1, 4, sibling).start())

    def relay_four(c):
        pl.when(has_earlier)(lambda: arrive(c, 4))
        pl.when(has_later)(lambda: move(c, 4, 8, 1, later).start())
        move(c, 4, 6 - 4 * side, 3 - side, across).start()
        move(c, 4, 5 - 2 * core, 5 - core, sibling).start()

    def relay_two_and_eight(c):
        arrive(c, 2)
        move(c, 2, 3 - 2 * core, 6, sibling).start()
        pl.when(has_earlier)(lambda: arrive(c, 8))
        pl.when(side == 1)(lambda: move(c, 8, 6, 3, across).start())
        pl.when(core == 1)(lambda: move(c, 8, 7, 5, sibling).start())

    def relay_six(c):
        arrive(c, 6)
        move(c, 6, 7 - 2 * core, 7, sibling).start()

    def gathered_all(c):
        for slot in (1, 3, 5, 7):
            arrive(c, slot)

    def gather_sent(c):
        for number in (0, 1):
            pl.when(has_later)(lambda: move(c, 0, 4, number, later).wait_send())
        for number in range(2, 8):
            move(c, 0, 2, number, across).wait_send()

    def give(c, source, number, device):
        return remote(
            source, landed.at[c, number], bsend.at[c, number], breceive.at[c, number], device
        )

    def got(c, number):
        give(c, grads.at[c, 0], number, sibling).wait_recv()

    is_core = core.astype(F32)
    is_side = side.astype(F32)

    def term(c, number):
        return landed[c, number].astype(F32)

    def give_siblings(c):
        for number, bottom, step in ((3, 5, 2), (1, 7, -2), (2, 1, 2), (0, 3, -2)):
            give(c, grads.at[c, bottom + step * core - 1], number, sibling).start()

    def give_across(c):
        got(c, 3)
        sums[c, 1] = (grads[c, 5].astype(F32) + term(c, 3)).astype(BF16)
        give(c, sums.at[c, 1], 5, across).start()
        got(c, 2)
        sums[c, 0] = (grads[c, 1].astype(F32) + term(c, 2)).astype(BF16)
        give(c, sums.at[c, 0], 4, across).start()

    def give_eight(c):
        got(c, 1)
        got(c, 5)
        total = grads[c, 7].astype(F32) + is_core * term(c, 1) + is_side * term(c, 5)
        sums[c, 3] = total.astype(BF16)
        pl.when(has_earlier)(lambda: give(c, sums.at[c, 3], 7, earlier).start())

    def give_four(c):
        got(c, 0)
        got(c, 4)
        total = grads[c, 3].astype(F32) + (1 - is_core) * term(c, 1) + is_core * term(c, 0)
        total = total + (1 - is_side) * term(c, 5) + is_side * term(c, 4)
        pl.when(has_later)(lambda: got(c, 7))
        total = total + term(c, 7)
        sums[c, 2] = total.astype(BF16)
        pl.when(has_earlier)(lambda: give(c, sums.at[c, 2], 6, earlier).start())

    def columns(c):
        return pl.ds(pl.multiple_of(c * LANES, LANES), LANES)

    def store(c, number, source, target):
        return pltpu.make_async_copy(source, target.at[:, columns(c)], stores.at[c, number])

    spread_token = lax.broadcasted_iota(jnp.int32, (tokens, pitch), 0)
    spread_row = lax.broadcasted_iota(jnp.int32, (tokens, pitch), 1)
    spread_inside = (spread_token >= spread_row * POOL) & (spread_token < spread_row * POOL + POOL)

    def finish(c):
        pl.when(has_later)(lambda: got(c, 6))
        total = (1 - is_core) * term(c, 0) + term(c, 6) + (1 - is_side) * term(c, 4)
        total = total.astype(BF16)
        spread = jnp.where(spread_inside, 1.0 / POOL, 0.0).astype(BF16)
        for which, target in enumerate((dk_out, dv_out)):
            shared = jnp.dot(spread, total[which], preferred_element_type=F32)
            out_buf[c, which] = (own[c, which] + shared).astype(BF16)
            store(c, which, out_buf.at[c, which], target).start()

    def given(c):
        for number in range(6):
            give(c, grads.at[c, 0], number, sibling).wait_send()
        for number in (6, 7):
            pl.when(has_earlier)(lambda: give(c, grads.at[c, 0], number, sibling).wait_send())

    def weight_out(n):
        mine = weights.at[head, pl.ds(core * half, half)]
        return remote(mine, mine, wsend.at[n - 1], wreceive.at[n - 1], peers[n - 1])

    def weight_on(n):
        theirs = weights.at[lax.rem(head + parts - n, parts), pl.ds(core * half, half)]
        return remote(theirs, theirs, fsend.at[n - 1], freceive.at[n - 1], sibling)

    def attended_out(c, n):
        return remote(
            att.at[lax.rem(head + n, parts), :, columns(c)], att_in.at[head, :, columns(c)],
            asend.at[c, n - 1], areceive.at[c, n - 1], peers[n - 1],
        )

    def mine(lane, h):
        return (lane < HEAD_DIM) if h == 0 else (lane >= HEAD_DIM)

    def lines(h):
        return slice(h * HEAD_DIM, (h + 1) * HEAD_DIM)

    def stacked(h, first, second):
        return jnp.concatenate([first, second] if h == 0 else [second, first], axis=0)

    spare_line = lax.broadcasted_iota(jnp.int32, (HEAD_DIM, tokens), 0)

    def query_side(c, h, level):
        spare = jnp.where(spare_line == 0, level, 0.0).astype(BF16)
        return stacked(h, query_t[c, lines(h), :], spare)

    def weighted(h, value_t, low):
        moving = jnp.concatenate([value_t, jnp.ones((16, low.shape[0]), BF16)], axis=0)
        return jnp.dot(moving, low, preferred_element_type=F32)

    def grad_sides(h, inverse, delta, c):
        side = (grad_t[c, lines(h), :] * inverse).astype(BF16)
        high = delta.astype(BF16).astype(F32)
        low = delta - high
        spare = jnp.where(spare_line == 0, -high, jnp.where(spare_line == 1, -low, 0.0)).astype(BF16)
        return stacked(h, side, spare)

    def marked(block, h, fill):
        lane = lax.broadcasted_iota(jnp.int32, block.shape, 1)
        return jnp.where(mine(lane, h), block, fill)

    def by_column(first, second):
        return lax.dot_general(first, second, BY_COLUMN, preferred_element_type=F32)

    def own_forward(c, carry):
        query_t[c] = (q[:, columns(c)] * scale).T
        key = k[:, columns(c)]
        key_own_t[c] = key.T
        value_t = v[:, columns(c)].T
        scores = [jnp.dot(key, query_side(c, h, 0.0), preferred_element_type=F32) for h in range(2)]
        for h in range(2):
            top = jnp.max(scores[h], axis=0, keepdims=True)
            own_peak[c, h : h + 1, :] = top
            low = jnp.exp(scores[h] - top).astype(BF16)
            own_probs[c, h] = low
            own_out[c, h] = weighted(h, value_t[lines(h), :], low)
        return carry

    def own_backward(c, carry):
        value = v[:, columns(c)]
        centred = []
        for h in range(2):
            centred.append(jnp.dot(marked(value, h, jnp.ones_like(value)), own_grad[c, h], preferred_element_type=F32))
        dk, dv, dq = [], [], []
        for h in range(2):
            low = own_probs[c, h]
            grad_scores = (low.astype(F32) * centred[h]).astype(BF16)
            dv.append(by_column(own_grad[c, h, lines(h), :], low))
            dk.append(by_column(query_t[c, lines(h), :], grad_scores))
            dq.append(jnp.dot(key_own_t[c, lines(h), :], grad_scores, preferred_element_type=F32))
        for which, parts_ in enumerate((dk, dv)):
            own[c, which] = jnp.concatenate(parts_, axis=0).T
        total = jnp.concatenate(dq, axis=0) + dq_part[c]
        dq_buf[c] = (total * scale).astype(BF16).T
        store(c, 2, dq_buf.at[c], dq_out).start()
        return carry

    for c in range(min(2, chunks)):
        send_own(c)
    inputs[2].wait()
    for n in range(1, parts):
        weight_out(n).start()
    inputs[3].wait()
    grad_t[...] = lax.dot_general(
        weights[head], grad[...], BY_COLUMN, preferred_element_type=F32
    ).reshape(grad_t.shape)
    inputs[4].wait()
    middle = chunks // 2
    lax.fori_loop(0, middle, own_forward, 0)
    relay_four(0)
    if chunks > 2:
        send_own(2)
    lax.fori_loop(middle, chunks, own_forward, 0)
    if chunks > 1:
        relay_four(1)
    for c in range(3, chunks):
        send_own(c)
    bias[...] = jnp.full(bias.shape, EXCLUDED, BF16)
    relay_two_and_eight(0)
    if chunks > 2:
        relay_four(2)
    if chunks > 1:
        relay_two_and_eight(1)
    relay_six(0)
    for c in range(3, chunks):
        relay_four(c)
    gathered_all(0)
    running = jnp.full((1, LANES), 1 - start[0], jnp.int32).astype(F32)
    for slot in range(MEM):
        keep_slot = mem[0, slot + 1, 0, pooled : pooled + 1, :].astype(F32)
        exists = mem[0, slot + 1, 0, pooled + 1 : pooled + 2, :].astype(F32)
        level = ((1.0 - running * exists) * EXCLUDED).astype(BF16)
        bias[slot * pitch : slot * pitch + pooled, :] = jnp.broadcast_to(level, (pooled, LANES))
        running = running * keep_slot

    def step(i, carry):
        @pl.when(i > 0)
        def _():
            gathered_all(i)

        for slot in range(MEM):
            rows_ = slice(slot * pitch, (slot + 1) * pitch)
            keys[rows_, :] = mem[i, slot + 1, 0]
            values[rows_, :] = mem[i, slot + 1, 1]
        key_t = keys[...].T
        value_t = values[...].T
        block = 2 * pitch
        blocks = [slice(n * block, (n + 1) * block) for n in range(MEM // 2)]
        count_ = len(blocks)
        scores, low, out, dq, gside, centred, gs = {}, {}, {}, {}, {}, {}, {}
        qside = [query_side(i, h, 1.0) for h in range(2)]
        top = [None, None]
        attended = [None, None]

        def score(h, n):
            key = marked(keys[blocks[n], :], h, bias[blocks[n], :])
            scores[h, n] = jnp.dot(key, qside[h], preferred_element_type=F32)

        def peak(h):
            best = own_peak[i, h : h + 1, :]
            for n in range(count_):
                best = jnp.maximum(best, jnp.max(scores[h, n], axis=0, keepdims=True))
            top[h] = best

        def expo(h, n):
            low[h, n] = jnp.exp(scores[h, n] - top[h]).astype(BF16)

        def mix(h, n):
            part = weighted(h, value_t[lines(h), blocks[n]], low[h, n])
            out[h] = part if n == 0 else out[h] + part

        def turn(h):
            shift = jnp.exp(own_peak[i, h : h + 1, :] - top[h])
            total = out[h] + own_out[i, h] * shift
            inverse = 1.0 / total[HEAD_DIM : HEAD_DIM + 1, :]
            attended[h] = total[:HEAD_DIM, :] * inverse
            side = (grad_t[i, lines(h), :] * inverse).astype(BF16)
            delta = jnp.sum(side.astype(F32) * attended[h], axis=0, keepdims=True)
            gside[h] = grad_sides(h, inverse, delta, i)
            own_grad[i, h] = grad_sides(h, inverse * shift, delta * shift, i)

        def centre(h, n):
            block_ = values[blocks[n], :]
            value = marked(block_, h, jnp.ones_like(block_))
            centred[h, n] = jnp.dot(value, gside[h], preferred_element_type=F32)

        def grad_score(h, n):
            gs[h, n] = (low[h, n].astype(F32) * centred[h, n]).astype(BF16)

        def value_grad(h, n):
            totals[1, lines(h), blocks[n]] = by_column(gside[h][lines(h), :], low[h, n])

        def key_grad(h, n):
            totals[0, lines(h), blocks[n]] = by_column(query_t[i, lines(h), :], gs[h, n])
            part = jnp.dot(key_t[lines(h), blocks[n]], gs[h, n], preferred_element_type=F32)
            dq[h] = part if n == 0 else dq[h] + part

        def give_block(n):
            for which in range(2):
                both = totals[which, :, blocks[n]].astype(BF16).T
                for slot in range(2):
                    grads[i, 2 * n + slot, which] = both[slot * pitch : (slot + 1) * pitch, :]

        for n in range(count_):
            score(0, n)
        peak(0)
        for n in range(count_):
            score(1, n)
            expo(0, n)
            if n > 0:
                mix(0, n - 1)
        mix(0, count_ - 1)
        peak(1)
        turn(0)

        @pl.when(i + 1 < chunks)
        def _():
            relay_six(i + 1)

        @pl.when(i + 2 < chunks)
        def _():
            relay_two_and_eight(i + 2)

        @pl.when(i > 0)
        def _():
            give_across(i - 1)

        @pl.when(i > 1)
        def _():
            give_eight(i - 2)

        @pl.when(i > 2)
        def _():
            give_four(i - 3)

        centre(0, 0)
        for n in range(count_):
            if n + 1 < count_:
                centre(0, n + 1)
            expo(1, n)
            value_grad(0, n)
            grad_score(0, n)
            mix(1, n)
            if n > 0:
                key_grad(0, n - 1)
        turn(1)
        key_grad(0, count_ - 1)
        both = jnp.concatenate(attended, axis=0).astype(BF16).T
        for part in range(parts):
            att[part, :, columns(i)] = both[part * rows : (part + 1) * rows, :]
        for n in range(1, parts):
            attended_out(i, n).start()

        centre(1, 0)
        for n in range(count_):
            if n + 1 < count_:
                centre(1, n + 1)
            value_grad(1, n)
            grad_score(1, n)
            if n > 0:
                key_grad(1, n - 1)
        key_grad(1, count_ - 1)
        for n in range(count_):
            give_block(n)
        give_siblings(i)
        dq_part[i] = jnp.concatenate([dq[0], dq[1]], axis=0)

        @pl.when(i == min(1, chunks - 1))
        def _():
            for n in range(1, parts):
                weight_out(n).wait_recv()
                weight_on(n).start()

        gather_sent(i)
        return carry

    lax.fori_loop(0, chunks, step, 0)

    last = chunks - 1
    if chunks > 1:
        give_eight(last - 1)
    if chunks > 2:
        give_four(last - 2)
    lax.fori_loop(0, middle, own_backward, 0)
    give_across(last)
    if chunks > 1:
        give_four(last - 1)
    lax.fori_loop(middle, chunks, own_backward, 0)
    for c in range(chunks - 2):
        finish(c)
    give_eight(last)
    total = jnp.dot(att[head], weights[head], preferred_element_type=F32)
    for n in range(1, parts):
        weight_on(n).wait_recv()
        for c in range(chunks):
            attended_out(c, n).wait_recv()
    for n in range(1, parts):
        other = lax.rem(head + n, parts)
        total = total + jnp.dot(att_in[other], weights[other], preferred_element_type=F32)
    projected_buf[...] = total.astype(BF16)
    final = pltpu.make_async_copy(projected_buf, projected, loads.at[5])
    final.start()
    if chunks > 1:
        finish(last - 1)
    give_four(last)
    for c in range(chunks - 1):
        given(c)
        for number in range(3):
            store(c, number, dq_buf.at[c], dq_out).wait()
    for n in range(1, parts):
        weight_out(n).wait_send()
        weight_on(n).wait_send()
        for c in range(chunks):
            attended_out(c, n).wait_send()
    finish(last)
    given(last)
    for number in range(3):
        store(last, number, dq_buf.at[last], dq_out).wait()
    final.wait()


def whole(queries, key_tokens, value_tokens, out_weight, out_grad, start, count, parts):
    tokens, width = queries.shape
    full = out_weight.shape[1]
    chunks = width // LANES
    rows = tokens // parts
    pitch = -(-(tokens // POOL + 2) // 8) * 8
    anywhere = pl.BlockSpec(memory_space=pl.ANY)
    dma = pltpu.SemaphoreType.DMA
    return pl.pallas_call(
        functools.partial(kernel, count, parts),
        in_specs=[pl.BlockSpec(memory_space=pltpu.SMEM)] + [anywhere] * 5,
        out_specs=[pl.BlockSpec(memory_space=pltpu.VMEM)] * 4,
        out_shape=[pltpu.VMEM(s_.shape, s_.dtype) for s_ in [
            jax.ShapeDtypeStruct((rows, full), BF16),
            jax.ShapeDtypeStruct((tokens, width), BF16),
            jax.ShapeDtypeStruct((tokens, width), BF16),
            jax.ShapeDtypeStruct((tokens, width), BF16),
        ]],
        scratch_shapes=[
            pltpu.VMEM((tokens, width), BF16),
            pltpu.VMEM((tokens, width), BF16),
            pltpu.VMEM((tokens, width), BF16),
            pltpu.VMEM((tokens, full), BF16),
            pltpu.VMEM((parts, width, full), BF16),
            pltpu.VMEM((chunks, MEM + 1, 2, pitch, LANES), BF16),
            pltpu.VMEM((MEM * pitch, LANES), BF16),
            pltpu.VMEM((MEM * pitch, LANES), BF16),
            pltpu.VMEM((MEM * pitch, LANES), BF16),
            pltpu.VMEM((chunks, LANES, tokens), F32),
            pltpu.VMEM((chunks, LANES, tokens), BF16),
            pltpu.VMEM((chunks, LANES, tokens), BF16),
            pltpu.VMEM((chunks, 2, tokens, tokens), BF16),
            pltpu.VMEM((chunks, 2, HEAD_DIM + 16, tokens), F32),
            pltpu.VMEM((chunks, 2, tokens), F32),
            pltpu.VMEM((chunks, 2, LANES, tokens), BF16),
            pltpu.VMEM((chunks, LANES, tokens), F32),
            pltpu.VMEM((chunks, 2, tokens, LANES), F32),
            pltpu.VMEM((chunks, MEM, 2, pitch, LANES), BF16),
            pltpu.VMEM((chunks, 8, 2, pitch, LANES), BF16),
            pltpu.VMEM((chunks, 4, 2, pitch, LANES), BF16),
            pltpu.VMEM((2, LANES, MEM * pitch), F32),
            pltpu.VMEM((parts, rows, width), BF16),
            pltpu.VMEM((parts, rows, width), BF16),
            pltpu.VMEM((chunks, tokens, LANES), BF16),
            pltpu.VMEM((chunks, 2, tokens, LANES), BF16),
            pltpu.VMEM((rows, full), BF16),
            dma((6,)),
            dma((chunks, 8)),
            dma((chunks, MEM + 1)),
            dma((chunks, 8)),
            dma((chunks, 8)),
            dma((parts - 1,)),
            dma((parts - 1,)),
            dma((parts - 1,)),
            dma((parts - 1,)),
            dma((chunks, parts - 1)),
            dma((chunks, parts - 1)),
            dma((chunks, 3)),
        ],
        compiler_params=pltpu.CompilerParams(collective_id=1, has_side_effects=True),
        name="attention",
    )(start, queries, key_tokens, value_tokens, out_weight, out_grad)


def local(queries, key_tokens, value_tokens, out_weight, out_grad, clip_starts):
    projected, dq, dk, dv = whole(
        queries[0], key_tokens[0], value_tokens[0], out_weight, out_grad[0], clip_starts,
        lax.axis_size("tm"), lax.axis_size("head"),
    )
    return (projected[None], dq[None], dk[None], dv[None])


def solution(mesh):
    return jax.shard_map(
        local,
        mesh=mesh,
        in_specs=(
            P("tm", None, "head"),
            P("tm", None, "head"),
            P("tm", None, "head"),
            P("head", None),
            P("tm", None, None),
            P("tm"),
        ),
        out_specs=(
            P("tm", "head", None),
            P("tm", None, "head"),
            P("tm", None, "head"),
            P("tm", None, "head"),
        ),
        check_vma=False,
    )
```

```python
import functools

import jax
import jax.numpy as jnp
from jax import lax
from jax.experimental import pallas as pl
from jax.experimental.pallas import tpu as pltpu
from jax.sharding import PartitionSpec as P

HEAD_DIM = 64
POOL = 4
MEM = 8
GROUP = 4
LANES = 2 * HEAD_DIM
EXCLUDED = -1e30
F32 = jnp.float32
BF16 = jnp.bfloat16
BY_COLUMN = (((1,), (1,)), ((), ()))
BY_ROW = (((0,), (0,)), ((), ()))


def remote(source, target, send, receive, device):
    return pltpu.make_async_remote_copy(
        src_ref=source,
        dst_ref=target,
        send_sem=send,
        recv_sem=receive,
        device_id=device,
        device_id_type=pl.DeviceIdType.MESH,
    )


def place(count):
    me = lax.axis_index("tm")
    core = lax.rem(me, 2)
    side = lax.rem(me // 2, 2)
    sibling = {"tm": me + 1 - 2 * core}
    across = {"tm": me + 2 - 4 * side}
    later = [{"tm": lax.rem(me + n * GROUP, count)} for n in (1, 2)]
    earlier = [{"tm": lax.rem(me + 2 * count - n * GROUP, count)} for n in (1, 2)]
    has_later = [me + n * GROUP < count for n in (1, 2)]
    has_earlier = [me >= n * GROUP for n in (1, 2)]
    return me, core, side, sibling, across, later, earlier, has_later, has_earlier


def kernel(
    count, parts, start, q_in, k_in, v_in, weight_in, grad_in,
    projected, dq_out, dk_out, dv_out,
    q, k, v, grad, weights, mem, keys, values, bias, grad_t,
    query_t, key_own_t, own_probs, own_out, own_peak, own_grad, dq_part,
    own, grads, landed_core, landed_side, landed_far, sums, totals, att, att_in,
    loads, gsend, greceive, bsend, breceive, wsend, wreceive, fsend, freceive,
    asend, areceive,
):
    me, core, side, sibling, across, later, earlier, has_later, has_earlier = place(count)
    head = lax.axis_index("head")
    tokens, width = q.shape
    full = grad.shape[1]
    chunks = width // LANES
    pooled = tokens // POOL
    pitch = mem.shape[3]
    base = MEM * pitch
    rows = tokens // parts
    half = width // 2
    scale = HEAD_DIM ** (-0.5)

    def load(number, source, target):
        return pltpu.make_async_copy(source, target, loads.at[number])

    inputs = [
        load(0, k_in, k), load(1, v_in, v), load(2, weight_in, weights.at[head]),
        load(3, grad_in, grad), load(4, q_in, q),
    ]
    for copy in inputs:
        copy.start()

    peers = [{"head": lax.rem(head + n, parts)} for n in range(1, parts)]
    barrier = pltpu.get_barrier_semaphore()
    neighbours = [sibling, across] + later + earlier + peers
    for device in neighbours:
        pl.semaphore_signal(barrier, inc=1, device_id=device, device_id_type=pl.DeviceIdType.MESH)

    row = lax.broadcasted_iota(jnp.int32, (pitch, tokens), 0)
    token = lax.broadcasted_iota(jnp.int32, (pitch, tokens), 1)
    inside = (token >= row * POOL) & (token < row * POOL + POOL)
    mixing = jnp.where(inside, 1.0 / POOL, 0.0).astype(BF16)
    line = lax.broadcasted_iota(jnp.int32, (pitch, width), 0)
    keep = jnp.full((pitch, width), 1 - start[0], jnp.int32).astype(F32)
    for which, ref in enumerate((k, v)):
        inputs[which].wait()
        mean = jnp.dot(mixing, ref[...], preferred_element_type=F32)
        mean = jnp.where(line == pooled, keep, jnp.where(line == pooled + 1, 1.0, mean)).astype(BF16)
        for c in range(chunks):
            mem[c, 0, which] = mean[:, c * LANES : (c + 1) * LANES]

    @pl.when(jnp.logical_not(has_earlier[0]))
    def _():
        for slot in (4, 8):
            for c in range(chunks):
                mem[c, slot] = jnp.zeros(mem.shape[2:], BF16)

    for n in range(2):
        @pl.when(jnp.logical_not(has_later[n]))
        def _():
            for c in range(chunks):
                for which in range(2):
                    landed_far[c, which, n] = jnp.zeros(landed_far.shape[3:], BF16)

    pl.semaphore_wait(barrier, len(neighbours))

    arrivals = {4: 0, 8: 1, 2: 2, 6: 3, 1: 4, 3: 4, 5: 4, 7: 4}

    def move(c, source, target, lane, arrival, device):
        return remote(
            mem.at[c, source], mem.at[c, target],
            gsend.at[c, lane], greceive.at[c, arrival], device,
        )

    def to_later(c, source, target):
        return move(c, source, target, 0, arrivals[target], later[0])

    def to_across(c, source, target, arrival):
        return move(c, source, target, 1, arrival, across)

    def to_sibling(c, source, target):
        return move(c, source, target, 2, 4, sibling)

    def arrive(c, slot):
        move(c, slot, slot, 0, arrivals[slot], sibling).wait_recv()

    def send_own(c):
        pl.when(has_later[0])(lambda: to_later(c, 0, 4).start())
        pl.when(side == 0)(lambda: to_across(c, 0, 2, 2).start())
        pl.when(core == 0)(lambda: to_sibling(c, 0, 1).start())

    def relay_four(c):
        pl.when(has_earlier[0])(lambda: arrive(c, 4))
        pl.when(has_later[0])(lambda: to_later(c, 4, 8).start())
        to_across(c, 4, 6 - 4 * side, 3 - side).start()
        to_sibling(c, 4, 5 - 2 * core).start()

    def relay_two_and_eight(c):
        arrive(c, 2)
        to_sibling(c, 2, 3 - 2 * core).start()
        pl.when(has_earlier[0])(lambda: arrive(c, 8))
        pl.when(side == 1)(lambda: to_across(c, 8, 6, 3).start())
        pl.when(core == 1)(lambda: to_sibling(c, 8, 7).start())

    def relay_six(c):
        arrive(c, 6)
        to_sibling(c, 6, 7 - 2 * core).start()

    def blocks_of(c, count_, lane, arrival):
        some = mem.at[c, pl.ds(0, count_)]
        return remote(some, some, gsend.at[c, lane], greceive.at[c, arrival], sibling)

    def gathered_all(c):
        blocks_of(c, 4, 2, 4).wait_recv()

    def gather_sent(c):
        pl.when(has_later[0])(lambda: blocks_of(c, 2, 0, 0).wait_send())
        blocks_of(c, 2, 1, 0).wait_send()
        blocks_of(c, 4, 2, 0).wait_send()

    def give(c, which, source, target, lane, device):
        return remote(source, target, bsend.at[c, lane], breceive.at[c, which, lane], device)

    def got(c, which, lane, target):
        give(c, which, target, target, lane, sibling).wait_recv()

    is_core = core.astype(F32)
    is_side = side.astype(F32)

    def give_siblings(c, which):
        give(c, which, grads.at[c, which, 0], landed_core.at[c, which], 0, sibling).start()

    def give_across(c, which):
        got(c, which, 0, landed_core.at[c, which])
        for n, slot in ((0, 0), (1, 2)):
            other = landed_core[c, which, 1 + slot - core].astype(F32)
            sums[c, which, n] = (grads[c, which, 1, slot].astype(F32) + other).astype(BF16)
        give(c, which, sums.at[c, which, pl.ds(0, 2)], landed_side.at[c, which], 1, across).start()

    def give_earlier(c, which):
        got(c, which, 1, landed_side.at[c, which])
        far = landed_side[c, which, 1].astype(F32)
        total = grads[c, which, 1, 3].astype(F32) + is_side * far
        sums[c, which, 3] = (total + is_core * landed_core[c, which, 3].astype(F32)).astype(BF16)
        pl.when(has_earlier[1])(
            lambda: give(
                c, which, sums.at[c, which, 3], landed_far.at[c, which, 1], 3, earlier[1]
            ).start()
        )
        total = grads[c, which, 1, 1].astype(F32) + landed_core[c, which, 2 - core].astype(F32)
        near = landed_side[c, which, 1 - side].astype(F32)
        sums[c, which, 2] = (total + near).astype(BF16)
        pl.when(has_earlier[0])(
            lambda: give(
                c, which, sums.at[c, which, 2], landed_far.at[c, which, 0], 2, earlier[0]
            ).start()
        )

    def columns(c):
        return pl.ds(pl.multiple_of(c * LANES, LANES), LANES)

    spread_token = lax.broadcasted_iota(jnp.int32, (pitch, tokens), 1)
    spread_row = lax.broadcasted_iota(jnp.int32, (pitch, tokens), 0)
    spread_inside = (spread_token >= spread_row * POOL) & (spread_token < spread_row * POOL + POOL)

    def finish(c, which):
        for n in range(2):
            pl.when(has_later[n])(lambda: got(c, which, 2 + n, landed_far.at[c, which, n]))
        total = (1 - is_core) * landed_core[c, which, 0].astype(F32)
        total = total + (1 - is_side) * landed_side[c, which, 0].astype(F32)
        for n in range(2):
            total = total + landed_far[c, which, n].astype(F32)
        total = total.astype(BF16)
        spread = jnp.where(spread_inside, 1.0 / POOL, 0.0).astype(BF16)
        shared = lax.dot_general(total, spread, BY_ROW, preferred_element_type=F32)
        target = (dk_out, dv_out)[which]
        target[:, columns(c)] = (own[c, which] + shared).astype(BF16).T

    def given(c):
        give(c, 0, landed_core.at[c], landed_core.at[c], 0, sibling).wait_send()
        give(c, 0, landed_side.at[c], landed_side.at[c], 1, sibling).wait_send()
        for n in range(2):
            pl.when(has_earlier[n])(
                lambda: give(c, 0, landed_far.at[c, 0], landed_far.at[c, 0], 2 + n, sibling).wait_send()
            )

    def weight_out(n):
        mine = weights.at[head, pl.ds(core * half, half)]
        return remote(mine, mine, wsend.at[n - 1], wreceive.at[n - 1], peers[n - 1])

    def weight_on(n):
        theirs = weights.at[lax.rem(head + parts - n, parts), pl.ds(core * half, half)]
        return remote(theirs, theirs, fsend.at[n - 1], freceive.at[n - 1], sibling)

    def attended_out(c, n):
        return remote(
            att.at[lax.rem(head + n, parts), :, columns(c)], att_in.at[head, :, columns(c)],
            asend.at[c, n - 1], areceive.at[c, n - 1], peers[n - 1],
        )

    def mine(lane, h):
        return (lane < HEAD_DIM) if h == 0 else (lane >= HEAD_DIM)

    def lines(h):
        return slice(h * HEAD_DIM, (h + 1) * HEAD_DIM)

    def stacked(h, first, second):
        return jnp.concatenate([first, second] if h == 0 else [second, first], axis=0)

    spare_line = lax.broadcasted_iota(jnp.int32, (16, tokens), 0)
    blank = jnp.zeros((HEAD_DIM - 16, tokens), BF16)

    def spared(first, second):
        lines_ = jnp.where(spare_line == 0, first, jnp.where(spare_line == 1, second, 0.0))
        return jnp.concatenate([lines_.astype(BF16), blank], axis=0)

    def query_side(c, h, level):
        return stacked(h, query_t[c, lines(h), :], spared(level, 0.0))

    def weighted(h, value_t, low):
        moving = jnp.concatenate([value_t, jnp.ones((16, low.shape[0]), BF16)], axis=0)
        return jnp.dot(moving, low, preferred_element_type=F32)

    def grad_sides(h, inverse, delta, c):
        side = (grad_t[c, lines(h), :] * inverse).astype(BF16)
        high = delta.astype(BF16).astype(F32)
        low = delta - high
        return stacked(h, side, spared(-high, -low))

    def marked(block, h, fill):
        lane = lax.broadcasted_iota(jnp.int32, block.shape, 1)
        return jnp.where(mine(lane, h), block, fill)

    def by_column(first, second):
        return lax.dot_general(first, second, BY_COLUMN, preferred_element_type=F32)

    def own_forward(cs):
        scores, value_t = {}, {}
        for c in cs:
            query_t[c] = (q[:, columns(c)] * scale).T
            key = k[:, columns(c)]
            key_own_t[c] = key.T
            value_t[c] = v[:, columns(c)].T
            for h in range(2):
                scores[c, h] = jnp.dot(key, query_side(c, h, 0.0), preferred_element_type=F32)
        for c in cs:
            for h in range(2):
                top = jnp.max(scores[c, h], axis=0, keepdims=True)
                own_peak[c, h : h + 1, :] = top
                low = jnp.exp(scores[c, h] - top).astype(BF16)
                own_probs[c, h] = low
                own_out[c, h] = weighted(h, value_t[c][lines(h), :], low)

    def own_backward(cs):
        heads = [(c, h) for c in cs for h in range(2)]
        centred, grad_scores, dq = {}, {}, {}

        def centre(c, h):
            value = marked(v[:, columns(c)], h, jnp.ones((tokens, LANES), BF16))
            centred[c, h] = jnp.dot(value, own_grad[c, h], preferred_element_type=F32)

        def scored(c, h):
            low = own_probs[c, h]
            grad_scores[c, h] = (low.astype(F32) * centred[c, h]).astype(BF16)
            own[c, 1, lines(h), :] = by_column(own_grad[c, h, lines(h), :], low)

        def spent(c, h):
            own[c, 0, lines(h), :] = by_column(query_t[c, lines(h), :], grad_scores[c, h])
            dq[h] = jnp.dot(key_own_t[c, lines(h), :], grad_scores[c, h], preferred_element_type=F32)
            if h == 1:
                total = jnp.concatenate([dq[0], dq[1]], axis=0) + dq_part[c]
                dq_out[:, columns(c)] = (total * scale).astype(BF16).T

        centre(*heads[0])
        for n, pair in enumerate(heads):
            if n + 1 < len(heads):
                centre(*heads[n + 1])
            scored(*pair)
            if n > 0:
                spent(*heads[n - 1])
        spent(*heads[-1])

    for c in range(min(2, chunks)):
        send_own(c)
    inputs[2].wait()
    for n in range(1, parts):
        weight_out(n).start()
    inputs[3].wait()
    grad_t[...] = lax.dot_general(
        weights[head], grad[...], BY_COLUMN, preferred_element_type=F32
    ).reshape(grad_t.shape)
    inputs[4].wait()
    middle = chunks // 2
    own_forward(range(middle, chunks))
    relay_four(0)
    if chunks > 2:
        send_own(2)
    own_forward(range(middle))
    if chunks > 1:
        relay_four(1)
    for c in range(3, chunks):
        send_own(c)
    bias[...] = jnp.full(bias.shape, EXCLUDED, BF16)
    relay_two_and_eight(0)
    if chunks > 2:
        relay_four(2)
    if chunks > 1:
        relay_two_and_eight(1)
    relay_six(0)
    for c in range(3, chunks):
        relay_four(c)
    gathered_all(0)
    running = jnp.full((1, LANES), 1 - start[0], jnp.int32).astype(F32)
    for slot in range(MEM):
        keep_slot = mem[0, slot + 1, 0, pooled : pooled + 1, :].astype(F32)
        exists = mem[0, slot + 1, 0, pooled + 1 : pooled + 2, :].astype(F32)
        level = ((1.0 - running * exists) * EXCLUDED).astype(BF16)
        bias[slot * pitch : slot * pitch + pooled, :] = jnp.broadcast_to(level, (pooled, LANES))
        running = running * keep_slot

    def step(i, carry):
        @pl.when(i > 0)
        def _():
            gathered_all(i)

        for slot in range(MEM):
            rows_ = slice(slot * pitch, (slot + 1) * pitch)
            keys[rows_, :] = mem[i, slot + 1, 0]
            values[rows_, :] = mem[i, slot + 1, 1]
        key_t = keys[...].T
        value_t = values[...].T
        block = 2 * pitch
        blocks = [slice(n * block, (n + 1) * block) for n in range(MEM // 2)]
        count_ = len(blocks)
        scores, low, out, dq, gside, centred, gs = {}, {}, {}, {}, {}, {}, {}
        qside = [query_side(i, h, 1.0) for h in range(2)]
        top = [None, None]
        attended = [None, None]

        def score(h, n):
            key = marked(keys[blocks[n], :], h, bias[blocks[n], :])
            scores[h, n] = jnp.dot(key, qside[h], preferred_element_type=F32)

        def peak(h):
            best = own_peak[i, h : h + 1, :]
            for n in range(count_):
                best = jnp.maximum(best, jnp.max(scores[h, n], axis=0, keepdims=True))
            top[h] = best

        def expo(h, n):
            low[h, n] = jnp.exp(scores[h, n] - top[h]).astype(BF16)

        def mix(h, n):
            part = weighted(h, value_t[lines(h), blocks[n]], low[h, n])
            out[h] = part if n == 0 else out[h] + part

        def turn(h):
            shift = jnp.exp(own_peak[i, h : h + 1, :] - top[h])
            total = out[h] + own_out[i, h] * shift
            inverse = 1.0 / total[HEAD_DIM : HEAD_DIM + 1, :]
            attended[h] = total[:HEAD_DIM, :] * inverse
            side = (grad_t[i, lines(h), :] * inverse).astype(BF16)
            delta = jnp.sum(side.astype(F32) * attended[h], axis=0, keepdims=True)
            gside[h] = grad_sides(h, inverse, delta, i)
            own_grad[i, h] = grad_sides(h, inverse * shift, delta * shift, i)

        def centre(h, n):
            block_ = values[blocks[n], :]
            value = marked(block_, h, jnp.ones_like(block_))
            centred[h, n] = jnp.dot(value, gside[h], preferred_element_type=F32)

        def grad_score(h, n):
            gs[h, n] = (low[h, n].astype(F32) * centred[h, n]).astype(BF16)

        def value_grad(h, n):
            totals[1, lines(h), blocks[n]] = by_column(gside[h][lines(h), :], low[h, n])

        def key_grad(h, n):
            totals[0, lines(h), blocks[n]] = by_column(query_t[i, lines(h), :], gs[h, n])
            part = jnp.dot(key_t[lines(h), blocks[n]], gs[h, n], preferred_element_type=F32)
            dq[h] = part if n == 0 else dq[h] + part

        def give_block(n, which):
            both = totals[which, :, blocks[n]].astype(BF16).T
            for slot in range(2):
                grads[i, which, slot, n] = both[slot * pitch : (slot + 1) * pitch, :]

        for n in range(count_):
            score(0, n)
        peak(0)
        for n in range(count_):
            score(1, n)
            expo(0, n)
            if n > 0:
                mix(0, n - 1)
        mix(0, count_ - 1)
        peak(1)
        turn(0)

        @pl.when(i + 1 < chunks)
        def _():
            relay_six(i + 1)

        @pl.when(i + 2 < chunks)
        def _():
            relay_two_and_eight(i + 2)

        @pl.when(i > 0)
        def _():
            for which in (1, 0):
                give_across(i - 1, which)

        @pl.when(i > 1)
        def _():
            for which in (1, 0):
                give_earlier(i - 2, which)

        centre(0, 0)
        for n in range(count_):
            if n + 1 < count_:
                centre(0, n + 1)
            expo(1, n)
            value_grad(0, n)
            grad_score(0, n)
            mix(1, n)
            if n > 0:
                key_grad(0, n - 1)
        turn(1)
        key_grad(0, count_ - 1)
        both = jnp.concatenate(attended, axis=0).astype(BF16).T
        for part in range(parts):
            att[part, :, columns(i)] = both[part * rows : (part + 1) * rows, :]
        for n in range(1, parts):
            attended_out(i, n).start()

        for n in range(count_):
            value_grad(1, n)
        centre(1, 0)
        for n in range(count_):
            give_block(n, 1)
        give_siblings(i, 1)
        for n in range(count_):
            if n + 1 < count_:
                centre(1, n + 1)
            grad_score(1, n)
            if n > 0:
                key_grad(1, n - 1)
                give_block(n - 1, 0)
        key_grad(1, count_ - 1)
        give_block(count_ - 1, 0)
        give_siblings(i, 0)
        dq_part[i] = jnp.concatenate([dq[0], dq[1]], axis=0)

        @pl.when(i == min(2, chunks - 1))
        def _():
            for n in range(1, parts):
                weight_out(n).wait_recv()
                weight_on(n).start()

        gather_sent(i)
        return carry

    lax.fori_loop(0, chunks, step, 0)

    last = chunks - 1
    own_backward(range(middle, chunks))
    for which in (1, 0):
        give_across(last, which)
    if chunks > 1:
        for which in (1, 0):
            give_earlier(last - 1, which)
    if middle > 0:
        own_backward(range(middle))
    total = jnp.dot(att[head], weights[head], preferred_element_type=F32)
    for which in (1, 0):
        give_earlier(last, which)
    for n in range(1, parts):
        weight_on(n).wait_recv()
        for c in range(chunks):
            attended_out(c, n).wait_recv()
    for n in range(1, parts):
        other = lax.rem(head + n, parts)
        total = total + jnp.dot(att_in[other], weights[other], preferred_element_type=F32)
    projected[...] = total.astype(BF16)
    for c in range(last):
        for which in (1, 0):
            finish(c, which)
        given(c)
    for n in range(1, parts):
        weight_out(n).wait_send()
        weight_on(n).wait_send()
        for c in range(chunks):
            attended_out(c, n).wait_send()
    for which in (1, 0):
        finish(last, which)
    given(last)


def whole(queries, key_tokens, value_tokens, out_weight, out_grad, start, count, parts):
    tokens, width = queries.shape
    full = out_weight.shape[1]
    chunks = width // LANES
    rows = tokens // parts
    pitch = -(-(tokens // POOL + 2) // 8) * 8
    anywhere = pl.BlockSpec(memory_space=pl.ANY)
    dma = pltpu.SemaphoreType.DMA
    return pl.pallas_call(
        functools.partial(kernel, count, parts),
        in_specs=[pl.BlockSpec(memory_space=pltpu.SMEM)] + [anywhere] * 5,
        out_specs=[pl.BlockSpec(memory_space=pltpu.VMEM)] * 4,
        out_shape=[pltpu.VMEM(s_.shape, s_.dtype) for s_ in [
            jax.ShapeDtypeStruct((rows, full), BF16),
            jax.ShapeDtypeStruct((tokens, width), BF16),
            jax.ShapeDtypeStruct((tokens, width), BF16),
            jax.ShapeDtypeStruct((tokens, width), BF16),
        ]],
        scratch_shapes=[
            pltpu.VMEM((tokens, width), BF16),
            pltpu.VMEM((tokens, width), BF16),
            pltpu.VMEM((tokens, width), BF16),
            pltpu.VMEM((tokens, full), BF16),
            pltpu.VMEM((parts, width, full), BF16),
            pltpu.VMEM((chunks, MEM + 1, 2, pitch, LANES), BF16),
            pltpu.VMEM((MEM * pitch, LANES), BF16),
            pltpu.VMEM((MEM * pitch, LANES), BF16),
            pltpu.VMEM((MEM * pitch, LANES), BF16),
            pltpu.VMEM((chunks, LANES, tokens), F32),
            pltpu.VMEM((chunks, LANES, tokens), BF16),
            pltpu.VMEM((chunks, LANES, tokens), BF16),
            pltpu.VMEM((chunks, 2, tokens, tokens), BF16),
            pltpu.VMEM((chunks, 2, HEAD_DIM + 16, tokens), F32),
            pltpu.VMEM((chunks, 2, tokens), F32),
            pltpu.VMEM((chunks, 2, LANES, tokens), BF16),
            pltpu.VMEM((chunks, LANES, tokens), F32),
            pltpu.VMEM((chunks, 2, LANES, tokens), F32),
            pltpu.VMEM((chunks, 2, 2, MEM // 2, pitch, LANES), BF16),
            pltpu.VMEM((chunks, 2, MEM // 2, pitch, LANES), BF16),
            pltpu.VMEM((chunks, 2, 2, pitch, LANES), BF16),
            pltpu.VMEM((chunks, 2, 2, pitch, LANES), BF16),
            pltpu.VMEM((chunks, 2, 4, pitch, LANES), BF16),
            pltpu.VMEM((2, LANES, MEM * pitch), F32),
            pltpu.VMEM((parts, rows, width), BF16),
            pltpu.VMEM((parts, rows, width), BF16),
            dma((5,)),
            dma((chunks, 3)),
            dma((chunks, 5)),
            dma((chunks, 4)),
            dma((chunks, 2, 4)),
            dma((parts - 1,)),
            dma((parts - 1,)),
            dma((parts - 1,)),
            dma((parts - 1,)),
            dma((chunks, parts - 1)),
            dma((chunks, parts - 1)),
        ],
        compiler_params=pltpu.CompilerParams(collective_id=1, has_side_effects=True),
        name="attention",
    )(start, queries, key_tokens, value_tokens, out_weight, out_grad)


def copy_kernel(*refs):
    count = len(refs) // 2
    done = refs[-1]
    copies = [pltpu.make_async_copy(refs[n], refs[count + n], done.at[n]) for n in range(count)]
    for copy in copies:
        copy.start()
    for copy in copies:
        copy.wait()


def copied(arrays):
    return pl.pallas_call(
        copy_kernel,
        in_specs=[pl.BlockSpec(memory_space=pltpu.VMEM)] * len(arrays),
        out_specs=[pl.BlockSpec(memory_space=pl.ANY)] * len(arrays),
        out_shape=[jax.ShapeDtypeStruct(array.shape, array.dtype) for array in arrays],
        scratch_shapes=[pltpu.SemaphoreType.DMA((len(arrays),))],
        name="copied",
    )(*[pltpu.with_memory_space_constraint(array, pltpu.VMEM) for array in arrays])


def local(queries, key_tokens, value_tokens, out_weight, out_grad, clip_starts):
    outputs = whole(
        queries[0], key_tokens[0], value_tokens[0], out_weight, out_grad[0], clip_starts,
        lax.axis_size("tm"), lax.axis_size("head"),
    )
    projected, dq, dk, dv = copied(outputs)
    return (projected[None], dq[None], dk[None], dv[None])


def solution(mesh):
    return jax.shard_map(
        local,
        mesh=mesh,
        in_specs=(
            P("tm", None, "head"),
            P("tm", None, "head"),
            P("tm", None, "head"),
            P("head", None),
            P("tm", None, None),
            P("tm"),
        ),
        out_specs=(
            P("tm", "head", None),
            P("tm", None, "head"),
            P("tm", None, "head"),
            P("tm", None, "head"),
        ),
        check_vma=False,
    )
```
